512 devices in a mesh: dp: 32 (over y_lo, z, core), expert: 16 (over y_hi, x).
Axes of the slice: x: 4, y: 8 (y_hi: 4, y_lo: 2; y = y_hi * 2 + y_lo), z: 8, core: 2. Of those that a mesh axis runs over, the one named last changes fastest.
Arguments:
- tokens: bfloat16 [65536, 2048], P(('dp', 'expert')), may hold values from -6 to 6
- routes: int32 [65536, 2], P(('dp', 'expert')), may hold values from 0 to 15, all different within a row; in each aligned block of 128 rows (0 to 127, 128 to 255, ...) at most 32 rows name the same one
- gate_values: float32 [65536, 2], P(('dp', 'expert')), may hold values from 0.1 to 1
- gate_weight: bfloat16 [16, 2048, 768], P('expert', 'dp'), may hold values from -0.125 to 0.125
- up_weight: bfloat16 [16, 2048, 768], P('expert', 'dp'), may hold values from -0.125 to 0.125
- down_weight: bfloat16 [16, 768, 2048], P('expert', None, 'dp'), may hold values from -0.21875 to 0.21875
Outputs:
- mixture: bfloat16 [65536, 2048], P(('dp', 'expert'))
The draws below stay inside these ranges and needn't reach their ends.
Inputs may be any that keep to these rules, and one draw needn't show every extreme that they name: `routes`: in the rows of one device no expert is named by more than 32 rows, and in every draw some device's rows name some expert exactly 32 times.
All inputs are finite; a program needn't handle non-finite values.
Results may differ from the reference program's by a relative error of at most 0.0057.
Values may be sent and summed in bfloat16 or wider, within the bound.
No kernel may reach another device: no remote copies, remote signals or barrier semaphores. Data moves between devices by JAX's collectives and lax.ppermute only.
A program may use at most 64 MiB of HBM per device.

```python
import math
import jax
import jax.numpy as jnp
import numpy as np

D = 2048
FF = 768
TOP = 2
TOK_DEV = 128
EXPERTS = 16
CAP = 32
TOKENS = 65536
N_DP = 32
N_EXPERT = 16


def block_scale(own_key, extent, pieces, smallest, top_value):
    def one(dim, blocks):
        draws = jax.random.uniform(jax.random.fold_in(jax.random.fold_in(own_key, 6), dim), (blocks,), jnp.float32, smallest / len(pieces), top_value / len(pieces))
        return jnp.repeat(jnp.exp(draws), extent[dim] // blocks).reshape((-1,) + (1,) * (len(extent) - dim - 1))

    level = one(*pieces[0])
    for cut in pieces[1:]:
        level = level * one(*cut)
    return level


def routed_block(rng, own, number, rows, number_of, top, bound, skew):
    order = jax.random.permutation(rng, number_of)
    packed, ordinary = load_shares(number_of, rows * top, bound, skew, True), load_shares(number_of, rows * top, bound, skew, False)
    places = jnp.arange(number_of)

    def named(lengths, offset_by):
        used = int((lengths > 0).sum())
        fixed = max(1, used // 4)
        moved = fixed + (places - fixed + offset_by * (used - fixed)) % max(1, number_of - fixed)
        return jnp.zeros((number_of,), jnp.int32).at[order[jnp.where(places < fixed, places, moved)]].set(jnp.asarray(lengths, jnp.int32))

    lengths = jnp.where(number % 4 == 0, named(packed, number // 4), named(ordinary, number - number // 4 - 1))
    mixed = jax.random.permutation(jax.random.fold_in(own, 3), number_of)
    giver, taker = mixed[0:number_of // 2 * 2:2], mixed[1:number_of // 2 * 2:2]
    margin = jnp.minimum(lengths[giver] - 1, bound - lengths[taker]) // 2
    margin = jnp.where((giver == order[0]) | (taker == order[0]) | (lengths[taker] == 0), 0, jnp.maximum(margin, 0))
    moved = jax.random.randint(jax.random.fold_in(own, 4), (number_of // 2,), 0, 1 << 20) % (margin + 1)
    lengths = lengths.at[giver].add(-moved).at[taker].add(moved)
    items = jnp.searchsorted(jnp.cumsum(lengths), jnp.arange(rows * top), side="right").astype(jnp.int32)
    listing = items.reshape(top, rows).T
    listing = listing[jax.random.permutation(jax.random.fold_in(own, 1), rows)]
    offset_by = jax.random.randint(jax.random.fold_in(own, 2), (rows, 1), 0, top)
    return jnp.take_along_axis(listing, (jnp.arange(top)[None, :] + offset_by) % top, axis=1)


def load_shares(number_of, total, most, skew, full):
    loads = [(1 << 20) // math.isqrt(standing ** skew) + 1 for standing in range(1, number_of + 1)]
    largest = most if full else min(most, max(-(-total // number_of), total * loads[0] // sum(loads)))
    least = 1 if total - largest >= number_of - 1 else 0
    counts, spare = [largest] + [least] * (number_of - 1), total - largest - least * (number_of - 1)
    while spare > 0:
        movable = [i for i in range(1, number_of) if counts[i] < largest] or [i for i in range(1, number_of) if counts[i] < most]
        whole, remaining = sum([loads[i] for i in movable]), spare
        for i in movable:
            more = min(most - counts[i], max(1, remaining * loads[i] // whole), spare)
            counts[i] = counts[i] + more
            spare = spare - more
    return np.array(counts)


def noise(key, dims, width, most, split=(), dtype=jnp.bfloat16):
    array = jax.random.normal(key, dims, jnp.float32) * width
    if len(split) > 0:
        array = block_scale(key, dims, split, -0.22, 0.18) * array
    return jnp.clip(array, min=-most, max=most).astype(dtype)


def setup_inputs(seed: int = 0) -> dict:
    splits = jax.random.split(jax.random.key(seed), 7)
    tokens = noise(splits[0], (TOKENS, D), 1.0, 6.0, ((0, 512),))
    routes_keys = jax.random.split(jax.random.fold_in(splits[1], 1), TOKENS // TOK_DEV)
    routes_turns = jax.random.permutation(jax.random.fold_in(splits[1], 3), TOKENS // TOK_DEV)
    routes = jax.vmap(lambda own, number: routed_block(jax.random.fold_in(splits[1], 2), own, number, TOK_DEV, EXPERTS, TOP, CAP, 2))(routes_keys, routes_turns).reshape((TOKENS, TOP))
    gate_values = jnp.clip(jnp.exp(math.log(1.0) - 2.3025851 * jax.random.uniform(splits[2], (TOKENS, TOP), jnp.float32) ** block_scale(splits[2], (TOKENS, TOP), ((0, 512),), -0.2, 0.2)), 0.1, 1.0)
    gate_weight = noise(splits[3], (EXPERTS, D, FF), D ** -0.5, 0.125, ((0, 16), (1, 32)))
    up_weight = noise(splits[4], (EXPERTS, D, FF), D ** -0.5, 0.125, ((0, 16), (1, 32)))
    down_weight = noise(splits[5], (EXPERTS, FF, D), FF ** -0.5, 0.21875, ((0, 16), (2, 32)))
    return {"tokens": tokens, "routes": routes, "gate_values": gate_values, "gate_weight": gate_weight, "up_weight": up_weight, "down_weight": down_weight}


def expert_output(selected, gate_weight, up_weight, down_weight):
    gated = jnp.dot(selected, gate_weight, preferred_element_type=jnp.float32)
    upward = jnp.dot(selected, up_weight, preferred_element_type=jnp.float32)
    hidden = (jax.nn.silu(gated) * upward).astype(jnp.bfloat16)
    return jnp.dot(hidden, down_weight, preferred_element_type=jnp.float32).astype(jnp.bfloat16)


def reference(tokens, routes, gate_values, gate_weight, up_weight, down_weight):
    flat_routes = routes.reshape(-1)
    slot_total = flat_routes.shape[0]
    row_bound = CAP * N_DP * N_EXPERT
    slot_results = jnp.zeros((slot_total, D), jnp.bfloat16)
    for expert in range(EXPERTS):
        positions = jnp.nonzero(flat_routes == expert, size=row_bound, fill_value=slot_total)[0].astype(jnp.int32)
        clipped = jnp.minimum(positions, slot_total - 1)
        selected = tokens[clipped // TOP]
        produced = expert_output(selected, gate_weight[expert], up_weight[expert], down_weight[expert])
        slot_results = slot_results.at[positions].set(produced, mode="drop")
    grouped = slot_results.reshape(-1, TOP, D)
    mixture = jnp.zeros((grouped.shape[0], D), jnp.float32)
    for column in range(TOP):
        mixture = mixture + gate_values[:, column:column + 1] * grouped[:, column, :].astype(jnp.float32)
    return mixture.astype(jnp.bfloat16)
```

```python
import jax
import jax.numpy as jnp
from jax import lax
from jax.experimental import pallas as pl
from jax.experimental.pallas import tpu as pltpu
from jax.sharding import PartitionSpec as P

F32 = jnp.float32
BF16 = jnp.bfloat16


def dot(a, b, dims=((1,), (0,))):
    return lax.dot_general(a, b, (dims, ((), ())), preferred_element_type=F32)


def dispatch_kernel(routes, gates, tokens, outgoing, high, low, *, capacity):
    slots = outgoing.shape[0]
    count = tokens.shape[0]
    top = routes.shape[0]
    slot = lax.broadcasted_iota(jnp.int32, (slots, count), 0)
    owner = slot // capacity
    place = (slot - owner * capacity).astype(F32)
    member = jnp.zeros((slots, count), F32)
    weight = jnp.zeros((slots, count), F32)
    for k in range(top):
        named = routes[k : k + 1, :] == owner
        member = jnp.where(named, 1.0, member)
        weight = jnp.where(named, gates[k : k + 1, :], weight)
    earlier = lax.broadcasted_iota(jnp.int32, (count, count), 0) < lax.broadcasted_iota(
        jnp.int32, (count, count), 1
    )
    rank = dot(member.astype(BF16), jnp.where(earlier, 1.0, 0.0).astype(BF16))
    chosen = jnp.where(rank == place, member, 0.0)
    outgoing[...] = dot(chosen.astype(BF16), tokens[...]).astype(BF16)
    weight = jnp.transpose(chosen * weight)
    rounded = weight.astype(BF16)
    high[...] = rounded
    low[...] = (weight - rounded.astype(F32)).astype(BF16)


def expert_kernel(rows, weights, produced, gate, up, down, hidden, sems, *, wide, shard):
    shards = weights.shape[0]
    inner = weights.shape[2]
    features = produced.shape[1]
    parts = (gate, up, down)
    copies = []
    for n in range(inner // wide):
        for p in range(2):
            copy = pltpu.make_async_copy(
                weights.at[:, p * shard : (p + 1) * shard, n * wide : (n + 1) * wide],
                parts[p].at[:, :, n * wide : (n + 1) * wide],
                sems.at[2 * n + p],
            )
            copy.start()
            copies.append(copy)
    last = pltpu.make_async_copy(
        weights.at[:, 2 * shard : 3 * shard, :], down, sems.at[2 * (inner // wide)]
    )
    last.start()
    x = rows[...]
    for n in range(inner // wide):
        columns = slice(n * wide, (n + 1) * wide)
        copies[2 * n].wait()
        copies[2 * n + 1].wait()
        gated = dot(x, gate[:, :, columns].reshape(shards * shard, wide))
        upward = dot(x, up[:, :, columns].reshape(shards * shard, wide))
        hidden[:, columns] = (gated / (1.0 + jnp.exp(-gated)) * upward).astype(BF16)
    last.wait()
    h = hidden[...]
    step = wide // shard
    for m in range(features // wide):
        part = down[m * step : (m + 1) * step].reshape(wide, inner)
        produced[:, m * wide : (m + 1) * wide] = dot(h, part, ((1,), (1,))).astype(BF16)


def combine_kernel(high, low, returned, mixture):
    rows = returned[...]
    mixture[...] = (dot(high[...], rows) + dot(low[...], rows)).astype(BF16)


def per_device(tokens, routes, gate_values, gate_weight, up_weight, down_weight):
    groups = lax.axis_size("expert")
    shards = lax.axis_size("dp")
    count, features = tokens.shape
    top = routes.shape[1]
    capacity = 2 * count * top // groups
    slots = groups * capacity
    _, shard, inner = gate_weight.shape
    joined = jnp.concatenate([gate_weight[0], up_weight[0], down_weight[0].T], axis=0)
    weights = lax.all_gather(joined, "dp", axis=0)
    outgoing, high, low = pl.pallas_call(
        lambda *refs: dispatch_kernel(*refs, capacity=capacity),
        out_shape=(
            jax.ShapeDtypeStruct((slots, features), BF16),
            jax.ShapeDtypeStruct((count, slots), BF16),
            jax.ShapeDtypeStruct((count, slots), BF16),
        ),
        name="dispatch",
    )(routes.T, gate_values.T, tokens)

    def exchange(rows):
        blocks = rows.reshape(groups, capacity, features)
        moved = lax.all_to_all(blocks, "expert", split_axis=0, concat_axis=0, tiled=True)
        return moved.reshape(slots, features)

    arrived = exchange(outgoing)
    wide = 256
    produced = pl.pallas_call(
        lambda *refs: expert_kernel(*refs, wide=wide, shard=shard),
        out_shape=jax.ShapeDtypeStruct((slots, features), BF16),
        in_specs=[
            pl.BlockSpec(memory_space=pltpu.VMEM),
            pl.BlockSpec(memory_space=pl.ANY),
        ],
        out_specs=pl.BlockSpec(memory_space=pltpu.VMEM),
        scratch_shapes=[
            pltpu.VMEM((shards, shard, inner), BF16),
            pltpu.VMEM((shards, shard, inner), BF16),
            pltpu.VMEM((shards, shard, inner), BF16),
            pltpu.VMEM((slots, inner), BF16),
            pltpu.SemaphoreType.DMA((2 * (inner // wide) + 1,)),
        ],
        name="expert",
    )(arrived, weights)
    returned = exchange(produced)
    return pl.pallas_call(
        combine_kernel,
        out_shape=jax.ShapeDtypeStruct((count, features), BF16),
        name="combine",
    )(high, low, returned)


def solution(mesh):
    placed = (
        P(("dp", "expert"), None),
        P(("dp", "expert"), None),
        P(("dp", "expert"), None),
        P("expert", "dp", None),
        P("expert", "dp", None),
        P("expert", None, "dp"),
    )
    return jax.shard_map(
        per_device, mesh=mesh, in_specs=placed, out_specs=P(("dp", "expert"), None), check_vma=False
    )
```

```python
import jax
import jax.numpy as jnp
from jax import lax
from jax.experimental import pallas as pl
from jax.experimental.pallas import tpu as pltpu
from jax.sharding import PartitionSpec as P

F32 = jnp.float32
BF16 = jnp.bfloat16


def dot(a, b, dims=((1,), (0,))):
    return lax.dot_general(a, b, (dims, ((), ())), preferred_element_type=F32)


def dispatch_kernel(routes, gates, tokens, outgoing, high, low, *, capacity):
    slots = outgoing.shape[0]
    count = tokens.shape[0]
    top = routes.shape[0]
    slot = lax.broadcasted_iota(jnp.int32, (slots, count), 0)
    owner = slot // capacity
    place = (slot - owner * capacity).astype(F32)
    member = jnp.zeros((slots, count), F32)
    weight = jnp.zeros((slots, count), F32)
    for k in range(top):
        named = routes[k : k + 1, :] == owner
        member = jnp.where(named, 1.0, member)
        weight = jnp.where(named, gates[k : k + 1, :], weight)
    earlier = lax.broadcasted_iota(jnp.int32, (count, count), 0) < lax.broadcasted_iota(
        jnp.int32, (count, count), 1
    )
    rank = dot(member.astype(BF16), jnp.where(earlier, 1.0, 0.0).astype(BF16))
    chosen = jnp.where(rank == place, member, 0.0)
    outgoing[...] = dot(chosen.astype(BF16), tokens[...]).astype(BF16)
    weight = jnp.transpose(chosen * weight)
    rounded = weight.astype(BF16)
    high[...] = rounded
    low[...] = (weight - rounded.astype(F32)).astype(BF16)


def expert_kernel(side, rows, weights, produced, x, gate, up, down, hidden, out, sems, *, wide, shard):
    members = weights.shape[0]
    inner = weights.shape[3]
    features = produced.shape[1]
    mine = side[0]
    sem = [0]

    def begin(source, target):
        copy = pltpu.make_async_copy(source, target, sems.at[sem[0]])
        sem[0] += 1
        copy.start()
        return copy

    def fetch(p, target, first, size):
        return [
            begin(
                weights.at[:, s, p * shard : (p + 1) * shard, first : first + size],
                target.at[
                    pl.ds((mine if s == 0 else 1 - mine) * members, members), :, first : first + size
                ],
            )
            for s in range(2)
        ]

    arrival = begin(rows, x)
    blocks = []
    for first in range(0, inner, wide):
        blocks.append(fetch(0, gate, first, wide) + fetch(1, up, first, wide))
    last = fetch(2, down, 0, inner)
    arrival.wait()
    for n, first in enumerate(range(0, inner, wide)):
        columns = slice(first, first + wide)
        for copy in blocks[n]:
            copy.wait()
        gated = dot(x[...], gate[:, :, columns].reshape(2 * members * shard, wide))
        upward = dot(x[...], up[:, :, columns].reshape(2 * members * shard, wide))
        hidden[:, columns] = (gated / (1.0 + jnp.exp(-gated)) * upward).astype(BF16)
    for copy in last:
        copy.wait()
    step = wide // shard
    leaving = []
    for m in range(features // wide):
        columns = slice(m * wide, (m + 1) * wide)
        part = down[m * step : (m + 1) * step].reshape(wide, inner)
        out[:, columns] = dot(hidden[...], part, ((1,), (1,))).astype(BF16)
        leaving.append(begin(out.at[:, columns], produced.at[:, columns]))
    for copy in leaving:
        copy.wait()


def combine_kernel(high, low, returned, mixture):
    rows = returned[...]
    mixture[...] = (dot(high[...], rows) + dot(low[...], rows)).astype(BF16)


def per_device(tokens, routes, gate_values, gate_weight, up_weight, down_weight):
    groups = lax.axis_size("expert")
    shards = lax.axis_size("dp")
    count, features = tokens.shape
    top = routes.shape[1]
    capacity = 2 * count * top // groups
    slots = groups * capacity
    _, shard, inner = gate_weight.shape
    joined = jnp.concatenate([gate_weight[0], up_weight[0], down_weight[0].T], axis=0)
    half = shards // 2
    swap = [(d, (d + half) % shards) for d in range(shards)]
    both = jnp.stack([joined, lax.ppermute(joined, "dp", swap)])
    sides = [list(range(half)), list(range(half, shards))]
    weights = lax.all_gather(both, "dp", axis=0, axis_index_groups=sides)
    side = (lax.axis_index("dp") // half).astype(jnp.int32).reshape(1)
    outgoing, high, low = pl.pallas_call(
        lambda *refs: dispatch_kernel(*refs, capacity=capacity),
        out_shape=(
            jax.ShapeDtypeStruct((slots, features), BF16),
            jax.ShapeDtypeStruct((count, slots), BF16),
            jax.ShapeDtypeStruct((count, slots), BF16),
        ),
        name="dispatch",
    )(routes.T, gate_values.T, tokens)

    def exchange(rows):
        blocks = rows.reshape(groups, capacity, features)
        moved = lax.all_to_all(blocks, "expert", split_axis=0, concat_axis=0, tiled=True)
        return moved.reshape(slots, features)

    arrived = exchange(outgoing)
    wide = 256
    anywhere = pl.BlockSpec(memory_space=pl.ANY)
    blocks = inner // wide
    produced = pl.pallas_call(
        lambda *refs: expert_kernel(*refs, wide=wide, shard=shard),
        out_shape=jax.ShapeDtypeStruct((slots, features), BF16),
        in_specs=[pl.BlockSpec(memory_space=pltpu.SMEM), anywhere, anywhere],
        out_specs=anywhere,
        scratch_shapes=[
            pltpu.VMEM((slots, features), BF16),
            pltpu.VMEM((shards, shard, inner), BF16),
            pltpu.VMEM((shards, shard, inner), BF16),
            pltpu.VMEM((shards, shard, inner), BF16),
            pltpu.VMEM((slots, inner), BF16),
            pltpu.VMEM((slots, features), BF16),
            pltpu.SemaphoreType.DMA((1 + 4 * blocks + 2 + features // wide,)),
        ],
        name="expert",
    )(side, arrived, weights)
    returned = exchange(produced)
    band = 512
    return pl.pallas_call(
        combine_kernel,
        out_shape=jax.ShapeDtypeStruct((count, features), BF16),
        grid=(features // band,),
        in_specs=[
            pl.BlockSpec((count, slots), lambda i: (0, 0)),
            pl.BlockSpec((count, slots), lambda i: (0, 0)),
            pl.BlockSpec((slots, band), lambda i: (0, i)),
        ],
        out_specs=pl.BlockSpec((count, band), lambda i: (0, i)),
        name="combine",
    )(high, low, returned)


def solution(mesh):
    placed = (
        P(("dp", "expert"), None),
        P(("dp", "expert"), None),
        P(("dp", "expert"), None),
        P("expert", "dp", None),
        P("expert", "dp", None),
        P("expert", None, "dp"),
    )
    return jax.shard_map(
        per_device, mesh=mesh, in_specs=placed, out_specs=P(("dp", "expert"), None), check_vma=False
    )
```

```python
import jax
import jax.numpy as jnp
from jax import lax
from jax.experimental import pallas as pl
from jax.experimental.pallas import tpu as pltpu
from jax.sharding import PartitionSpec as P

F32 = jnp.float32
BF16 = jnp.bfloat16


def dot(a, b, dims=((1,), (0,))):
    return lax.dot_general(a, b, (dims, ((), ())), preferred_element_type=F32)


def dispatch_kernel(routes, gates, tokens, outgoing, factors, *, capacity):
    slots = outgoing.shape[0]
    count = tokens.shape[0]
    top = routes.shape[0]
    slot = lax.broadcasted_iota(jnp.int32, (slots, count), 0)
    owner = slot // capacity
    place = (slot - owner * capacity).astype(F32)
    member = jnp.zeros((slots, count), F32)
    weight = jnp.zeros((slots, count), F32)
    for k in range(top):
        named = routes[k : k + 1, :] == owner
        member = jnp.where(named, 1.0, member)
        weight = jnp.where(named, gates[k : k + 1, :], weight)
    earlier = lax.broadcasted_iota(jnp.int32, (count, count), 0) < lax.broadcasted_iota(
        jnp.int32, (count, count), 1
    )
    rank = dot(member.astype(BF16), jnp.where(earlier, 1.0, 0.0).astype(BF16))
    chosen = jnp.where(rank == place, member, 0.0)
    outgoing[...] = dot(chosen.astype(BF16), tokens[...]).astype(BF16)
    weight = jnp.transpose(chosen * weight)
    rounded = weight.astype(BF16)
    factors[:count, :] = rounded
    factors[count:, :] = (weight - rounded.astype(F32)).astype(BF16)


def expert_kernel(
    place, rows, weights, near, far, produced, x, gate, up, down, hidden, out, sems, *, wide, shard, ring
):
    members = weights.shape[0]
    inner = weights.shape[3]
    features = produced.shape[1]
    mine, z, core = place[0], place[1], place[2]
    sem = [0]

    def begin(source, target):
        copy = pltpu.make_async_copy(source, target, sems.at[sem[0]])
        sem[0] += 1
        copy.start()
        return copy

    def side(s):
        return mine if s == 0 else 1 - mine

    def fetch(p, target, first):
        return [
            begin(
                weights.at[:, s, p * shard : (p + 1) * shard, first : first + wide],
                target.at[pl.ds(side(s) * members, members), :, first : first + wide],
            )
            for s in range(2)
        ]

    arrival = begin(rows, x)
    blocks = []
    for first in range(0, inner, wide):
        blocks.append(fetch(0, gate, first) + fetch(1, up, first))
    last = []
    for o in range(ring):
        from_z = lax.rem(z + (ring - o), ring)
        for source, from_core in ((near, core), (far, 1 - core)):
            for s in range(2):
                block = side(s) * members + from_z * 2 + from_core
                last.append(begin(source.at[o, s], down.at[block]))
    arrival.wait()
    for n, first in enumerate(range(0, inner, wide)):
        columns = slice(first, first + wide)
        for copy in blocks[n]:
            copy.wait()
        gated = dot(x[...], gate[:, :, columns].reshape(2 * members * shard, wide))
        upward = dot(x[...], up[:, :, columns].reshape(2 * members * shard, wide))
        hidden[:, columns] = (gated / (1.0 + jnp.exp(-gated)) * upward).astype(BF16)
    for copy in last:
        copy.wait()
    step = wide // shard
    leaving = []
    for m in range(features // wide):
        columns = slice(m * wide, (m + 1) * wide)
        part = down[m * step : (m + 1) * step].reshape(wide, inner)
        out[:, columns] = dot(hidden[...], part, ((1,), (1,))).astype(BF16)
        leaving.append(begin(out.at[:, columns], produced.at[:, columns]))
    for copy in leaving:
        copy.wait()


def combine_kernel(factors, returned, mixture):
    count = mixture.shape[0]
    sums = dot(factors[...], returned[...])
    mixture[...] = (sums[:count] + sums[count:]).astype(BF16)


def per_device(tokens, routes, gate_values, gate_weight, up_weight, down_weight):
    groups = lax.axis_size("expert")
    shards = lax.axis_size("dp")
    count, features = tokens.shape
    top = routes.shape[1]
    capacity = 2 * count * top // groups
    slots = groups * capacity
    _, shard, inner = gate_weight.shape
    half = shards // 2
    ring = half // 2
    joined = jnp.concatenate([gate_weight[0], up_weight[0], down_weight[0].T], axis=0)
    swap = [(d, (d + half) % shards) for d in range(shards)]
    other = lax.ppermute(joined, "dp", swap)
    outgoing, factors = pl.pallas_call(
        lambda *refs: dispatch_kernel(*refs, capacity=capacity),
        out_shape=(
            jax.ShapeDtypeStruct((slots, features), BF16),
            jax.ShapeDtypeStruct((2 * count, slots), BF16),
        ),
        name="dispatch",
    )(routes.T, gate_values.T, tokens)
    other, outgoing = lax.optimization_barrier((other, outgoing))
    sides = [list(range(half)), list(range(half, shards))]
    both = jnp.stack([joined[: 2 * shard], other[: 2 * shard]])
    weights = lax.all_gather(both, "dp", axis=0, axis_index_groups=sides)
    own = jnp.stack([joined[2 * shard :], other[2 * shard :]])

    def along(step):
        return [
            (d, d // half * half + (d % half // 2 + step) % ring * 2 + d % 2) for d in range(shards)
        ]

    ahead, behind = [own], [own]
    for k in range(ring // 2):
        ahead.append(lax.ppermute(ahead[-1], "dp", along(1)))
        if k < ring // 2 - 1:
            behind.append(lax.ppermute(behind[-1], "dp", along(-1)))
    near = jnp.stack(ahead + behind[:0:-1])
    far = lax.ppermute(near, "dp", [(d, d ^ 1) for d in range(shards)])
    index = lax.axis_index("dp").astype(jnp.int32)
    place = jnp.stack([index // half, index % half // 2, index % 2])

    def exchange(rows):
        blocks = rows.reshape(groups, capacity, features)
        moved = lax.all_to_all(blocks, "expert", split_axis=0, concat_axis=0, tiled=True)
        return moved.reshape(slots, features)

    arrived = exchange(outgoing)
    wide = 256
    anywhere = pl.BlockSpec(memory_space=pl.ANY)
    blocks = inner // wide
    anywhere = pl.BlockSpec(memory_space=pl.ANY)
    blocks = inner // wide
    produced = pl.pallas_call(
        lambda *refs: expert_kernel(*refs, wide=wide, shard=shard, ring=ring),
        out_shape=jax.ShapeDtypeStruct((slots, features), BF16),
        in_specs=[pl.BlockSpec(memory_space=pltpu.SMEM)] + [anywhere] * 4,
        out_specs=anywhere,
        scratch_shapes=[
            pltpu.VMEM((slots, features), BF16),
            pltpu.VMEM((shards, shard, inner), BF16),
            pltpu.VMEM((shards, shard, inner), BF16),
            pltpu.VMEM((shards, shard, inner), BF16),
            pltpu.VMEM((slots, inner), BF16),
            pltpu.VMEM((slots, features), BF16),
            pltpu.SemaphoreType.DMA((1 + 4 * blocks + shards + features // wide,)),
        ],
        name="expert",
    )(place, arrived, weights, near, far)
    returned = exchange(produced)
    return pl.pallas_call(
        combine_kernel,
        out_shape=jax.ShapeDtypeStruct((count, features), BF16),
        name="combine",
    )(factors, returned)


def solution(mesh):
    placed = (
        P(("dp", "expert"), None),
        P(("dp", "expert"), None),
        P(("dp", "expert"), None),
        P("expert", "dp", None),
        P("expert", "dp", None),
        P("expert", None, "dp"),
    )
    return jax.shard_map(
        per_device, mesh=mesh, in_specs=placed, out_specs=P(("dp", "expert"), None), check_vma=False
    )
```

```python
import jax
import jax.numpy as jnp
from jax import lax
from jax.experimental import pallas as pl
from jax.experimental.pallas import tpu as pltpu
from jax.sharding import PartitionSpec as P

F32 = jnp.float32
BF16 = jnp.bfloat16


def dot(a, b, dims=((1,), (0,))):
    return lax.dot_general(a, b, (dims, ((), ())), preferred_element_type=F32)


def dispatch_kernel(routes, gates, tokens, outgoing, factors, *, capacity):
    slots = outgoing.shape[0]
    count = tokens.shape[0]
    top = routes.shape[0]
    slot = lax.broadcasted_iota(jnp.int32, (slots, count), 0)
    owner = slot // capacity
    place = (slot - owner * capacity).astype(F32)
    member = jnp.zeros((slots, count), F32)
    weight = jnp.zeros((slots, count), F32)
    for k in range(top):
        named = routes[k : k + 1, :] == owner
        member = jnp.where(named, 1.0, member)
        weight = jnp.where(named, gates[k : k + 1, :], weight)
    earlier = lax.broadcasted_iota(jnp.int32, (count, count), 0) < lax.broadcasted_iota(
        jnp.int32, (count, count), 1
    )
    rank = dot(member.astype(BF16), jnp.where(earlier, 1.0, 0.0).astype(BF16))
    chosen = jnp.where(rank == place, member, 0.0)
    outgoing[...] = dot(chosen.astype(BF16), tokens[...]).astype(BF16)
    weight = jnp.transpose(chosen * weight)
    rounded = weight.astype(BF16)
    factors[:count, :] = rounded
    factors[count:, :] = (weight - rounded.astype(F32)).astype(BF16)


def start_copy(source, target, sems, used):
    copy = pltpu.make_async_copy(source, target, sems.at[len(used)])
    copy.start()
    used.append(copy)
    return copy


def project(hidden, down, out, produced, sems, used, wide):
    inner = down.shape[2]
    step = wide // down.shape[1]
    leaving = []
    for m in range(produced.shape[1] // wide):
        columns = slice(m * wide, (m + 1) * wide)
        part = down[m * step : (m + 1) * step].reshape(wide, inner)
        out[:, columns] = dot(hidden[...], part, ((1,), (1,))).astype(BF16)
        leaving.append(start_copy(out.at[:, columns], produced.at[:, columns], sems, used))
    return leaving


def expert_kernel(side, rows, weights, produced, passed, x, gate, up, down, hidden, out, sems, *, wide, shard):
    members = weights.shape[0]
    inner = weights.shape[2]
    used = []
    mine = side[0]

    def fetch(p, target, first):
        return [
            start_copy(
                weights.at[:, (2 * s + p) * shard : (2 * s + p + 1) * shard, first : first + wide],
                target.at[
                    pl.ds((mine if s == 0 else 1 - mine) * members, members), :, first : first + wide
                ],
                sems,
                used,
            )
            for s in range(2)
        ]

    arrival = start_copy(rows, x, sems, used)
    blocks = []
    for first in range(0, inner, wide):
        blocks.append(fetch(0, gate, first) + fetch(1, up, first))
    last = start_copy(weights.at[:, 4 * shard : 5 * shard, :], down, sems, used)
    arrival.wait()
    for n, first in enumerate(range(0, inner, wide)):
        columns = slice(first, first + wide)
        for copy in blocks[n]:
            copy.wait()
        gated = dot(x[...], gate[:, :, columns].reshape(2 * members * shard, wide))
        upward = dot(x[...], up[:, :, columns].reshape(2 * members * shard, wide))
        hidden[:, columns] = (gated / (1.0 + jnp.exp(-gated)) * upward).astype(BF16)
    leaving = [start_copy(hidden, passed, sems, used)]
    last.wait()
    leaving += project(hidden, down, out, produced, sems, used, wide)
    for copy in leaving:
        copy.wait()


def down_kernel(passed, weights, produced, down, hidden, out, sems, *, wide):
    used = []
    arrivals = [start_copy(passed, hidden, sems, used), start_copy(weights, down, sems, used)]
    for copy in arrivals:
        copy.wait()
    for copy in project(hidden, down, out, produced, sems, used, wide):
        copy.wait()


def combine_kernel(factors, returned, *rest):
    mixture = rest[-1]
    count = mixture.shape[0]
    sums = dot(factors[...], returned[...])
    mixture[...] = (sums[:count] + sums[count:]).astype(BF16)


def per_device(tokens, routes, gate_values, gate_weight, up_weight, down_weight):
    groups = lax.axis_size("expert")
    shards = lax.axis_size("dp")
    count, features = tokens.shape
    top = routes.shape[1]
    capacity = 2 * count * top // groups
    slots = groups * capacity
    _, shard, inner = gate_weight.shape
    half = shards // 2
    joined = jnp.concatenate([gate_weight[0], up_weight[0], down_weight[0].T], axis=0)
    swap = [(d, (d + half) % shards) for d in range(shards)]
    other = lax.ppermute(joined, "dp", swap)
    outgoing, factors = pl.pallas_call(
        lambda *refs: dispatch_kernel(*refs, capacity=capacity),
        out_shape=(
            jax.ShapeDtypeStruct((slots, features), BF16),
            jax.ShapeDtypeStruct((2 * count, slots), BF16),
        ),
        name="dispatch",
    )(routes.T, gate_values.T, tokens)
    other, outgoing = lax.optimization_barrier((other, outgoing))
    sides = [list(range(half)), list(range(half, shards))]
    side = (lax.axis_index("dp") // half).astype(jnp.int32)
    own_down, other_down = joined[2 * shard :], other[2 * shard :]
    first_down = jnp.where(side == 0, own_down, other_down)
    second_down = jnp.where(side == 0, other_down, own_down)
    early = jnp.concatenate([joined[: 2 * shard], other[: 2 * shard], first_down], axis=0)
    weights = lax.all_gather(early, "dp", axis=0, axis_index_groups=sides)
    late = lax.all_gather(second_down, "dp", axis=0, axis_index_groups=sides)

    def exchange(rows, name):
        with jax.named_scope(name):
            blocks = rows.reshape(groups, capacity, rows.shape[1])
            moved = lax.all_to_all(blocks, "expert", split_axis=0, concat_axis=0, tiled=True)
            return moved.reshape(rows.shape)

    arrived = exchange(outgoing, "outward")
    wide = 256
    blocks = inner // wide
    part = features // 2
    anywhere = pl.BlockSpec(memory_space=pl.ANY)
    produced, passed = pl.pallas_call(
        lambda *refs: expert_kernel(*refs, wide=wide, shard=shard),
        out_shape=(
            jax.ShapeDtypeStruct((slots, part), BF16),
            jax.ShapeDtypeStruct((slots, inner), BF16),
        ),
        in_specs=[pl.BlockSpec(memory_space=pltpu.SMEM), anywhere, anywhere],
        out_specs=(anywhere, anywhere),
        scratch_shapes=[
            pltpu.VMEM((slots, features), BF16),
            pltpu.VMEM((shards, shard, inner), BF16),
            pltpu.VMEM((shards, shard, inner), BF16),
            pltpu.VMEM((half, shard, inner), BF16),
            pltpu.VMEM((slots, inner), BF16),
            pltpu.VMEM((slots, part), BF16),
            pltpu.SemaphoreType.DMA((3 + 4 * blocks + part // wide,)),
        ],
        name="expert",
    )(side.reshape(1), arrived, weights)
    first = exchange(produced, "first")
    with jax.named_scope("rest"):
        produced = pl.pallas_call(
            lambda *refs: down_kernel(*refs, wide=wide),
            out_shape=jax.ShapeDtypeStruct((slots, part), BF16),
            in_specs=[anywhere, anywhere],
            out_specs=anywhere,
            scratch_shapes=[
                pltpu.VMEM((half, shard, inner), BF16),
                pltpu.VMEM((slots, inner), BF16),
                pltpu.VMEM((slots, part), BF16),
                pltpu.SemaphoreType.DMA((2 + part // wide,)),
            ],
            name="down",
        )(passed, late)
    second = exchange(produced, "second")
    whole = pl.BlockSpec((2 * count, slots), lambda i: (0, 0))
    rows = pl.BlockSpec((slots, part), lambda i: (0, 0))
    mixture = pl.pallas_call(
        combine_kernel,
        out_shape=jax.ShapeDtypeStruct((count, features), BF16),
        grid=(1,),
        in_specs=[whole, rows],
        out_specs=pl.BlockSpec((count, part), lambda i: (0, 0)),
        name="combine_first",
    )(factors, first)
    return pl.pallas_call(
        combine_kernel,
        out_shape=jax.ShapeDtypeStruct((count, features), BF16),
        grid=(1,),
        in_specs=[whole, rows, anywhere],
        out_specs=pl.BlockSpec((count, part), lambda i: (0, 1)),
        input_output_aliases={2: 0},
        name="combine_second",
    )(factors, second, mixture)


def solution(mesh):
    placed = (
        P(("dp", "expert"), None),
        P(("dp", "expert"), None),
        P(("dp", "expert"), None),
        P("expert", "dp", None),
        P("expert", "dp", None),
        P("expert", None, "dp"),
    )
    return jax.shard_map(
        per_device, mesh=mesh, in_specs=placed, out_specs=P(("dp", "expert"), None), check_vma=False
    )
```

```python
import jax
import jax.numpy as jnp
from jax import lax
from jax.experimental import pallas as pl
from jax.experimental.pallas import tpu as pltpu
from jax.sharding import PartitionSpec as P

F32 = jnp.float32
BF16 = jnp.bfloat16


def dot(a, b, dims=((1,), (0,))):
    return lax.dot_general(a, b, (dims, ((), ())), preferred_element_type=F32)


def dispatch_kernel(routes, gates, tokens, outgoing, factors, *, capacity):
    slots = outgoing.shape[0]
    count = tokens.shape[0]
    top = routes.shape[0]
    slot = lax.broadcasted_iota(jnp.int32, (slots, count), 0)
    owner = slot // capacity
    place = (slot - owner * capacity).astype(F32)
    member = jnp.zeros((slots, count), F32)
    weight = jnp.zeros((slots, count), F32)
    for k in range(top):
        named = routes[k : k + 1, :] == owner
        member = jnp.where(named, 1.0, member)
        weight = jnp.where(named, gates[k : k + 1, :], weight)
    earlier = lax.broadcasted_iota(jnp.int32, (count, count), 0) < lax.broadcasted_iota(
        jnp.int32, (count, count), 1
    )
    rank = dot(member.astype(BF16), jnp.where(earlier, 1.0, 0.0).astype(BF16))
    chosen = jnp.where(rank == place, member, 0.0)
    outgoing[...] = dot(chosen.astype(BF16), tokens[...]).astype(BF16)
    weight = jnp.transpose(chosen * weight)
    rounded = weight.astype(BF16)
    factors[:count, :] = rounded
    factors[count:, :] = (weight - rounded.astype(F32)).astype(BF16)


def expert_kernel(side, rows, weights, produced, x, gate, up, down, hidden, out, sems, *, wide, shard):
    members = weights.shape[0]
    inner = weights.shape[3]
    features = produced.shape[1]
    mine = side[0]
    sem = [0]

    def begin(source, target):
        copy = pltpu.make_async_copy(source, target, sems.at[sem[0]])
        sem[0] += 1
        copy.start()
        return copy

    def fetch(p, target, first, size):
        return [
            begin(
                weights.at[:, s, p * shard : (p + 1) * shard, first : first + size],
                target.at[
                    pl.ds((mine if s == 0 else 1 - mine) * members, members), :, first : first + size
                ],
            )
            for s in range(2)
        ]

    arrival = begin(rows, x)
    blocks = []
    for first in range(0, inner, wide):
        blocks.append(fetch(0, gate, first, wide) + fetch(1, up, first, wide))
    last = fetch(2, down, 0, inner)
    arrival.wait()
    for n, first in enumerate(range(0, inner, wide)):
        columns = slice(first, first + wide)
        for copy in blocks[n]:
            copy.wait()
        gated = dot(x[...], gate[:, :, columns].reshape(2 * members * shard, wide))
        upward = dot(x[...], up[:, :, columns].reshape(2 * members * shard, wide))
        hidden[:, columns] = (gated / (1.0 + jnp.exp(-gated)) * upward).astype(BF16)
    for copy in last:
        copy.wait()
    step = wide // shard
    leaving = []
    for m in range(features // wide):
        columns = slice(m * wide, (m + 1) * wide)
        part = down[m * step : (m + 1) * step].reshape(wide, inner)
        out[:, columns] = dot(hidden[...], part, ((1,), (1,))).astype(BF16)
        leaving.append(begin(out.at[:, columns], produced.at[:, columns]))
    for copy in leaving:
        copy.wait()


def combine_kernel(factors, returned, mixture):
    count = mixture.shape[0]
    sums = dot(factors[...], returned[...])
    mixture[...] = (sums[:count] + sums[count:]).astype(BF16)


def per_device(tokens, routes, gate_values, gate_weight, up_weight, down_weight):
    groups = lax.axis_size("expert")
    shards = lax.axis_size("dp")
    count, features = tokens.shape
    top = routes.shape[1]
    capacity = 2 * count * top // groups
    slots = groups * capacity
    _, shard, inner = gate_weight.shape
    half = shards // 2
    joined = jnp.concatenate([gate_weight[0], up_weight[0], down_weight[0].T], axis=0)
    swap = [(d, (d + half) % shards) for d in range(shards)]
    other = lax.ppermute(joined, "dp", swap)
    outgoing, factors = pl.pallas_call(
        lambda *refs: dispatch_kernel(*refs, capacity=capacity),
        out_shape=(
            jax.ShapeDtypeStruct((slots, features), BF16),
            jax.ShapeDtypeStruct((2 * count, slots), BF16),
        ),
        name="dispatch",
    )(routes.T, gate_values.T, tokens)
    other, outgoing = lax.optimization_barrier((other, outgoing))
    sides = [list(range(half)), list(range(half, shards))]
    both = jnp.stack([joined, other])
    weights = lax.all_gather(both, "dp", axis=0, axis_index_groups=sides)
    side = (lax.axis_index("dp") // half).astype(jnp.int32).reshape(1)

    def exchange(rows):
        blocks = rows.reshape(groups, capacity, features)
        moved = lax.all_to_all(blocks, "expert", split_axis=0, concat_axis=0, tiled=True)
        return moved.reshape(slots, features)

    arrived = exchange(outgoing)
    wide = 256
    anywhere = pl.BlockSpec(memory_space=pl.ANY)
    blocks = inner // wide
    anywhere = pl.BlockSpec(memory_space=pl.ANY)
    blocks = inner // wide
    produced = pl.pallas_call(
        lambda *refs: expert_kernel(*refs, wide=wide, shard=shard),
        out_shape=jax.ShapeDtypeStruct((slots, features), BF16),
        in_specs=[pl.BlockSpec(memory_space=pltpu.SMEM), anywhere, anywhere],
        out_specs=anywhere,
        scratch_shapes=[
            pltpu.VMEM((slots, features), BF16),
            pltpu.VMEM((shards, shard, inner), BF16),
            pltpu.VMEM((shards, shard, inner), BF16),
            pltpu.VMEM((shards, shard, inner), BF16),
            pltpu.VMEM((slots, inner), BF16),
            pltpu.VMEM((slots, features), BF16),
            pltpu.SemaphoreType.DMA((1 + 4 * blocks + 2 + features // wide,)),
        ],
        name="expert",
    )(side, arrived, weights)
    returned = exchange(produced)
    return pl.pallas_call(
        combine_kernel,
        out_shape=jax.ShapeDtypeStruct((count, features), BF16),
        name="combine",
    )(factors, returned)


def solution(mesh):
    placed = (
        P(("dp", "expert"), None),
        P(("dp", "expert"), None),
        P(("dp", "expert"), None),
        P("expert", "dp", None),
        P("expert", "dp", None),
        P("expert", None, "dp"),
    )
    return jax.shard_map(
        per_device, mesh=mesh, in_specs=placed, out_specs=P(("dp", "expert"), None), check_vma=False
    )
```

```python
import jax
import jax.numpy as jnp
from jax import lax
from jax.experimental import pallas as pl
from jax.experimental.pallas import tpu as pltpu
from jax.sharding import PartitionSpec as P

F32 = jnp.float32
BF16 = jnp.bfloat16


def dot(a, b, dims=((1,), (0,))):
    return lax.dot_general(a, b, (dims, ((), ())), preferred_element_type=F32)


def dispatch_kernel(routes, gates, tokens, outgoing, factors, *, capacity):
    slots = outgoing.shape[0]
    count = tokens.shape[0]
    top = routes.shape[0]
    slot = lax.broadcasted_iota(jnp.int32, (slots, count), 0)
    owner = slot // capacity
    place = (slot - owner * capacity).astype(F32)
    member = jnp.zeros((slots, count), F32)
    weight = jnp.zeros((slots, count), F32)
    for k in range(top):
        named = routes[k : k + 1, :] == owner
        member = jnp.where(named, 1.0, member)
        weight = jnp.where(named, gates[k : k + 1, :], weight)
    earlier = lax.broadcasted_iota(jnp.int32, (count, count), 0) < lax.broadcasted_iota(
        jnp.int32, (count, count), 1
    )
    rank = dot(member.astype(BF16), jnp.where(earlier, 1.0, 0.0).astype(BF16))
    chosen = jnp.where(rank == place, member, 0.0)
    outgoing[...] = dot(chosen.astype(BF16), tokens[...]).astype(BF16)
    weight = jnp.transpose(chosen * weight)
    rounded = weight.astype(BF16)
    factors[:count, :] = rounded
    factors[count:, :] = (weight - rounded.astype(F32)).astype(BF16)


def expert_kernel(side, rows, weights, produced, x, gate, up, down, hidden, out, sems, *, wide, shard):
    members = weights.shape[0]
    inner = weights.shape[3]
    features = produced.shape[1]
    mine = side[0]
    sem = [0]

    def begin(source, target):
        copy = pltpu.make_async_copy(source, target, sems.at[sem[0]])
        sem[0] += 1
        copy.start()
        return copy

    def fetch(p, target, first, size):
        return [
            begin(
                weights.at[:, s, p * shard : (p + 1) * shard, first : first + size],
                target.at[
                    pl.ds((mine if s == 0 else 1 - mine) * members, members), :, first : first + size
                ],
            )
            for s in range(2)
        ]

    arrival = begin(rows, x)
    blocks = []
    for first in range(0, inner, wide):
        blocks.append(fetch(0, gate, first, wide) + fetch(1, up, first, wide))
    last = fetch(2, down, 0, inner)
    arrival.wait()
    for n, first in enumerate(range(0, inner, wide)):
        columns = slice(first, first + wide)
        for copy in blocks[n]:
            copy.wait()
        gated = dot(x[...], gate[:, :, columns].reshape(2 * members * shard, wide))
        upward = dot(x[...], up[:, :, columns].reshape(2 * members * shard, wide))
        hidden[:, columns] = (gated / (1.0 + jnp.exp(-gated)) * upward).astype(BF16)
    for copy in last:
        copy.wait()
    step = wide // shard
    leaving = []
    for m in range(features // wide):
        columns = slice(m * wide, (m + 1) * wide)
        part = down[m * step : (m + 1) * step].reshape(wide, inner)
        out[:, columns] = dot(hidden[...], part, ((1,), (1,))).astype(BF16)
        leaving.append(begin(out.at[:, columns], produced.at[:, columns]))
    for copy in leaving:
        copy.wait()


def combine_kernel(factors, returned, mixture):
    count = mixture.shape[0]
    sums = dot(factors[...], returned[...])
    mixture[...] = (sums[:count] + sums[count:]).astype(BF16)


def per_device(tokens, routes, gate_values, gate_weight, up_weight, down_weight):
    groups = lax.axis_size("expert")
    shards = lax.axis_size("dp")
    count, features = tokens.shape
    top = routes.shape[1]
    capacity = 2 * count * top // groups
    slots = groups * capacity
    _, shard, inner = gate_weight.shape
    half = shards // 2
    joined = jnp.concatenate([gate_weight[0], up_weight[0], down_weight[0].T], axis=0)
    swap = [(d, (d + half) % shards) for d in range(shards)]
    other = lax.ppermute(joined, "dp", swap)
    outgoing, factors = pl.pallas_call(
        lambda *refs: dispatch_kernel(*refs, capacity=capacity),
        out_shape=(
            jax.ShapeDtypeStruct((slots, features), BF16),
            jax.ShapeDtypeStruct((2 * count, slots), BF16),
        ),
        name="dispatch",
    )(routes.T, gate_values.T, tokens)
    other, outgoing = lax.optimization_barrier((other, outgoing))
    sides = [list(range(half)), list(range(half, shards))]
    both = jnp.stack([joined, other])
    weights = lax.all_gather(both, "dp", axis=0, axis_index_groups=sides)
    side = (lax.axis_index("dp") // half).astype(jnp.int32).reshape(1)

    circles = [
        [
            ((b if e < groups // 2 else 1 - b) * half + i) * groups + e
            for e in range(groups)
        ]
        for b in range(2)
        for i in range(half)
    ]

    def exchange(rows):
        blocks = rows.reshape(groups, capacity, features)
        moved = lax.all_to_all(
            blocks,
            ("dp", "expert"),
            split_axis=0,
            concat_axis=0,
            tiled=True,
            axis_index_groups=circles,
        )
        return moved.reshape(slots, features)

    arrived = exchange(outgoing)
    wide = 256
    anywhere = pl.BlockSpec(memory_space=pl.ANY)
    blocks = inner // wide
    anywhere = pl.BlockSpec(memory_space=pl.ANY)
    blocks = inner // wide
    produced = pl.pallas_call(
        lambda *refs: expert_kernel(*refs, wide=wide, shard=shard),
        out_shape=jax.ShapeDtypeStruct((slots, features), BF16),
        in_specs=[pl.BlockSpec(memory_space=pltpu.SMEM), anywhere, anywhere],
        out_specs=anywhere,
        scratch_shapes=[
            pltpu.VMEM((slots, features), BF16),
            pltpu.VMEM((shards, shard, inner), BF16),
            pltpu.VMEM((shards, shard, inner), BF16),
            pltpu.VMEM((shards, shard, inner), BF16),
            pltpu.VMEM((slots, inner), BF16),
            pltpu.VMEM((slots, features), BF16),
            pltpu.SemaphoreType.DMA((1 + 4 * blocks + 2 + features // wide,)),
        ],
        name="expert",
    )(side, arrived, weights)
    returned = exchange(produced)
    return pl.pallas_call(
        combine_kernel,
        out_shape=jax.ShapeDtypeStruct((count, features), BF16),
        name="combine",
    )(factors, returned)


def solution(mesh):
    placed = (
        P(("dp", "expert"), None),
        P(("dp", "expert"), None),
        P(("dp", "expert"), None),
        P("expert", "dp", None),
        P("expert", "dp", None),
        P("expert", None, "dp"),
    )
    return jax.shard_map(
        per_device, mesh=mesh, in_specs=placed, out_specs=P(("dp", "expert"), None), check_vma=False
    )
```

```python
import jax
import jax.numpy as jnp
from jax import lax
from jax.experimental import pallas as pl
from jax.experimental.pallas import tpu as pltpu
from jax.sharding import PartitionSpec as P

F32 = jnp.float32
BF16 = jnp.bfloat16


def dot(a, b, dims=((1,), (0,))):
    return lax.dot_general(a, b, (dims, ((), ())), preferred_element_type=F32)


def dispatch_kernel(routes, gates, tokens, outgoing, factors, *, capacity):
    slots = outgoing.shape[0]
    count = tokens.shape[0]
    top = routes.shape[0]
    slot = lax.broadcasted_iota(jnp.int32, (slots, count), 0)
    owner = slot // capacity
    place = (slot - owner * capacity).astype(F32)
    member = jnp.zeros((slots, count), F32)
    weight = jnp.zeros((slots, count), F32)
    for k in range(top):
        named = routes[k : k + 1, :] == owner
        member = jnp.where(named, 1.0, member)
        weight = jnp.where(named, gates[k : k + 1, :], weight)
    earlier = lax.broadcasted_iota(jnp.int32, (count, count), 0) < lax.broadcasted_iota(
        jnp.int32, (count, count), 1
    )
    rank = dot(member.astype(BF16), jnp.where(earlier, 1.0, 0.0).astype(BF16))
    chosen = jnp.where(rank == place, member, 0.0)
    outgoing[...] = dot(chosen.astype(BF16), tokens[...]).astype(BF16)
    weight = jnp.transpose(chosen * weight)
    rounded = weight.astype(BF16)
    factors[:count, :] = rounded
    factors[count:, :] = (weight - rounded.astype(F32)).astype(BF16)


def expert_kernel(side, rows, weights, produced, x, gate, up, down, hidden, out, sems, *, wide, shard):
    members = weights.shape[0]
    inner = weights.shape[3]
    features = produced.shape[1]
    mine = side[0]
    sem = [0]

    def begin(source, target):
        copy = pltpu.make_async_copy(source, target, sems.at[sem[0]])
        sem[0] += 1
        copy.start()
        return copy

    cuts = [(first, wide) for first in range(0, inner, wide)]

    def fetch(p, target, first, size):
        return [
            begin(
                weights.at[:, s, p * shard : (p + 1) * shard, first : first + size],
                target.at[
                    pl.ds((mine if s == 0 else 1 - mine) * members, members), :, first : first + size
                ],
            )
            for s in range(2)
        ]

    arrival = begin(rows, x)
    blocks = []
    for first, size in cuts:
        blocks.append(fetch(0, gate, first, size) + fetch(1, up, first, size))
    last = fetch(2, down, 0, inner)
    arrival.wait()
    for n, (first, size) in enumerate(cuts):
        columns = slice(first, first + size)
        for copy in blocks[n]:
            copy.wait()
        gated = dot(x[...], gate[:, :, columns].reshape(2 * members * shard, size))
        upward = dot(x[...], up[:, :, columns].reshape(2 * members * shard, size))
        hidden[:, columns] = (gated / (1.0 + jnp.exp(-gated)) * upward).astype(BF16)
    for copy in last:
        copy.wait()
    step = wide // shard
    leaving = []
    for m in range(features // wide):
        columns = slice(m * wide, (m + 1) * wide)
        part = down[m * step : (m + 1) * step].reshape(wide, inner)
        out[:, columns] = dot(hidden[...], part, ((1,), (1,))).astype(BF16)
        leaving.append(begin(out.at[:, columns], produced.at[:, columns]))
    for copy in leaving:
        copy.wait()


def combine_kernel(factors, returned, mixture, rows, out, sems, *, band):
    count, features = mixture.shape
    bands = [slice(first, first + band) for first in range(0, features, band)]
    arriving = []
    for i, columns in enumerate(bands):
        copy = pltpu.make_async_copy(returned.at[:, columns], rows.at[:, columns], sems.at[i])
        copy.start()
        arriving.append(copy)
    leaving = []
    for i, columns in enumerate(bands):
        arriving[i].wait()
        sums = dot(factors[...], rows[:, columns])
        out[:, columns] = (sums[:count] + sums[count:]).astype(BF16)
        copy = pltpu.make_async_copy(
            out.at[:, columns], mixture.at[:, columns], sems.at[len(bands) + i]
        )
        copy.start()
        leaving.append(copy)
    for copy in leaving:
        copy.wait()


def per_device(tokens, routes, gate_values, gate_weight, up_weight, down_weight):
    groups = lax.axis_size("expert")
    shards = lax.axis_size("dp")
    count, features = tokens.shape
    top = routes.shape[1]
    capacity = 2 * count * top // groups
    slots = groups * capacity
    _, shard, inner = gate_weight.shape
    half = shards // 2
    joined = jnp.concatenate([gate_weight[0], up_weight[0], down_weight[0].T], axis=0)
    swap = [(d, (d + half) % shards) for d in range(shards)]
    other = lax.ppermute(joined, "dp", swap)
    outgoing, factors = pl.pallas_call(
        lambda *refs: dispatch_kernel(*refs, capacity=capacity),
        out_shape=(
            jax.ShapeDtypeStruct((slots, features), BF16),
            jax.ShapeDtypeStruct((2 * count, slots), BF16),
        ),
        name="dispatch",
    )(routes.T, gate_values.T, tokens)
    other, outgoing = lax.optimization_barrier((other, outgoing))
    sides = [list(range(half)), list(range(half, shards))]
    both = jnp.stack([joined, other])
    weights = lax.all_gather(both, "dp", axis=0, axis_index_groups=sides)
    side = (lax.axis_index("dp") // half).astype(jnp.int32).reshape(1)

    circles = [
        [
            ((b if e < groups // 2 else 1 - b) * half + i) * groups + e
            for e in range(groups)
        ]
        for b in range(2)
        for i in range(half)
    ]

    def exchange(rows):
        blocks = rows.reshape(groups, capacity, features)
        moved = lax.all_to_all(
            blocks,
            ("dp", "expert"),
            split_axis=0,
            concat_axis=0,
            tiled=True,
            axis_index_groups=circles,
        )
        return moved.reshape(slots, features)

    arrived = exchange(outgoing)
    wide = 256
    anywhere = pl.BlockSpec(memory_space=pl.ANY)
    anywhere = pl.BlockSpec(memory_space=pl.ANY)
    produced = pl.pallas_call(
        lambda *refs: expert_kernel(*refs, wide=wide, shard=shard),
        out_shape=jax.ShapeDtypeStruct((slots, features), BF16),
        in_specs=[pl.BlockSpec(memory_space=pltpu.SMEM), anywhere, anywhere],
        out_specs=anywhere,
        scratch_shapes=[
            pltpu.VMEM((slots, features), BF16),
            pltpu.VMEM((shards, shard, inner), BF16),
            pltpu.VMEM((shards, shard, inner), BF16),
            pltpu.VMEM((shards, shard, inner), BF16),
            pltpu.VMEM((slots, inner), BF16),
            pltpu.VMEM((slots, features), BF16),
            pltpu.SemaphoreType.DMA((1 + 4 * (inner // wide) + 2 + features // wide,)),
        ],
        name="expert",
    )(side, arrived, weights)
    returned = exchange(produced)
    band = 512
    return pl.pallas_call(
        lambda *refs: combine_kernel(*refs, band=band),
        out_shape=jax.ShapeDtypeStruct((count, features), BF16),
        in_specs=[pl.BlockSpec(memory_space=pltpu.VMEM), anywhere],
        out_specs=anywhere,
        scratch_shapes=[
            pltpu.VMEM((slots, features), BF16),
            pltpu.VMEM((count, features), BF16),
            pltpu.SemaphoreType.DMA((2 * (features // band),)),
        ],
        name="combine",
    )(factors, returned)


def solution(mesh):
    placed = (
        P(("dp", "expert"), None),
        P(("dp", "expert"), None),
        P(("dp", "expert"), None),
        P("expert", "dp", None),
        P("expert", "dp", None),
        P("expert", None, "dp"),
    )
    return jax.shard_map(
        per_device, mesh=mesh, in_specs=placed, out_specs=P(("dp", "expert"), None), check_vma=False
    )
```

```python
import jax
import jax.numpy as jnp
from jax import lax
from jax.experimental import pallas as pl
from jax.experimental.pallas import tpu as pltpu
from jax.sharding import PartitionSpec as P

F32 = jnp.float32
BF16 = jnp.bfloat16


def dot(a, b, dims=((1,), (0,))):
    return lax.dot_general(a, b, (dims, ((), ())), preferred_element_type=F32)


def dispatch_kernel(routes, gates, tokens, outgoing, factors, *, capacity):
    slots = outgoing.shape[0]
    count = tokens.shape[0]
    top = routes.shape[0]
    slot = lax.broadcasted_iota(jnp.int32, (slots, count), 0)
    owner = slot // capacity
    place = (slot - owner * capacity).astype(F32)
    member = jnp.zeros((slots, count), F32)
    weight = jnp.zeros((slots, count), F32)
    for k in range(top):
        named = routes[k : k + 1, :] == owner
        member = jnp.where(named, 1.0, member)
        weight = jnp.where(named, gates[k : k + 1, :], weight)
    earlier = lax.broadcasted_iota(jnp.int32, (count, count), 0) < lax.broadcasted_iota(
        jnp.int32, (count, count), 1
    )
    rank = dot(member.astype(BF16), jnp.where(earlier, 1.0, 0.0).astype(BF16))
    chosen = jnp.where(rank == place, member, 0.0)
    outgoing[...] = dot(chosen.astype(BF16), tokens[...]).astype(BF16)
    weight = jnp.transpose(chosen * weight)
    rounded = weight.astype(BF16)
    factors[:count, :] = rounded
    factors[count:, :] = (weight - rounded.astype(F32)).astype(BF16)


def expert_kernel(side, x, weights, produced, gate, up, down, hidden, out, sems, *, wide, shard):
    members = weights.shape[0]
    inner = weights.shape[3]
    features = produced.shape[1]
    mine = side[0]
    sem = [0]

    def begin(source, target):
        copy = pltpu.make_async_copy(source, target, sems.at[sem[0]])
        sem[0] += 1
        copy.start()
        return copy

    def fetch(p, target, first, size):
        return [
            begin(
                weights.at[:, s, p * shard : (p + 1) * shard, first : first + size],
                target.at[
                    pl.ds((mine if s == 0 else 1 - mine) * members, members), :, first : first + size
                ],
            )
            for s in range(2)
        ]

    blocks = []
    for first in range(0, inner, wide):
        blocks.append(fetch(0, gate, first, wide) + fetch(1, up, first, wide))
    last = fetch(2, down, 0, inner)
    for n, first in enumerate(range(0, inner, wide)):
        columns = slice(first, first + wide)
        for copy in blocks[n]:
            copy.wait()
        gated = dot(x[...], gate[:, :, columns].reshape(2 * members * shard, wide))
        upward = dot(x[...], up[:, :, columns].reshape(2 * members * shard, wide))
        hidden[:, columns] = (gated / (1.0 + jnp.exp(-gated)) * upward).astype(BF16)
    for copy in last:
        copy.wait()
    step = wide // shard
    leaving = []
    for m in range(features // wide):
        columns = slice(m * wide, (m + 1) * wide)
        part = down[m * step : (m + 1) * step].reshape(wide, inner)
        out[:, columns] = dot(hidden[...], part, ((1,), (1,))).astype(BF16)
        leaving.append(begin(out.at[:, columns], produced.at[:, columns]))
    for copy in leaving:
        copy.wait()


def combine_kernel(factors, returned, mixture):
    count = mixture.shape[0]
    sums = dot(factors[...], returned[...])
    mixture[...] = (sums[:count] + sums[count:]).astype(BF16)


def per_device(tokens, routes, gate_values, gate_weight, up_weight, down_weight):
    groups = lax.axis_size("expert")
    shards = lax.axis_size("dp")
    count, features = tokens.shape
    top = routes.shape[1]
    capacity = 2 * count * top // groups
    slots = groups * capacity
    _, shard, inner = gate_weight.shape
    half = shards // 2
    joined = jnp.concatenate([gate_weight[0], up_weight[0], down_weight[0].T], axis=0)
    swap = [(d, (d + half) % shards) for d in range(shards)]
    other = lax.ppermute(joined, "dp", swap)
    outgoing, factors = pl.pallas_call(
        lambda *refs: dispatch_kernel(*refs, capacity=capacity),
        out_shape=(
            jax.ShapeDtypeStruct((slots, features), BF16),
            jax.ShapeDtypeStruct((2 * count, slots), BF16),
        ),
        name="dispatch",
    )(routes.T, gate_values.T, tokens)
    other, outgoing = lax.optimization_barrier((other, outgoing))
    sides = [list(range(half)), list(range(half, shards))]
    both = jnp.stack([joined, other])
    weights = lax.all_gather(both, "dp", axis=0, axis_index_groups=sides)
    side = (lax.axis_index("dp") // half).astype(jnp.int32).reshape(1)

    circles = [
        [
            ((b if e < groups // 2 else 1 - b) * half + i) * groups + e
            for e in range(groups)
        ]
        for b in range(2)
        for i in range(half)
    ]

    def exchange(rows):
        blocks = rows.reshape(groups, capacity, features)
        moved = lax.all_to_all(
            blocks,
            ("dp", "expert"),
            split_axis=0,
            concat_axis=0,
            tiled=True,
            axis_index_groups=circles,
        )
        return pltpu.with_memory_space_constraint(moved.reshape(slots, features), pltpu.VMEM)

    arrived = exchange(outgoing)
    wide = 256
    anywhere = pl.BlockSpec(memory_space=pl.ANY)
    near = pl.BlockSpec(memory_space=pltpu.VMEM)
    blocks = inner // wide
    anywhere = pl.BlockSpec(memory_space=pl.ANY)
    near = pl.BlockSpec(memory_space=pltpu.VMEM)
    blocks = inner // wide
    produced = pl.pallas_call(
        lambda *refs: expert_kernel(*refs, wide=wide, shard=shard),
        out_shape=jax.ShapeDtypeStruct((slots, features), BF16),
        in_specs=[pl.BlockSpec(memory_space=pltpu.SMEM), near, anywhere],
        out_specs=anywhere,
        scratch_shapes=[
            pltpu.VMEM((shards, shard, inner), BF16),
            pltpu.VMEM((shards, shard, inner), BF16),
            pltpu.VMEM((shards, shard, inner), BF16),
            pltpu.VMEM((slots, inner), BF16),
            pltpu.VMEM((slots, features), BF16),
            pltpu.SemaphoreType.DMA((4 * blocks + 2 + features // wide,)),
        ],
        name="expert",
    )(side, arrived, weights)
    returned = exchange(produced)
    return pl.pallas_call(
        combine_kernel,
        out_shape=jax.ShapeDtypeStruct((count, features), BF16),
        name="combine",
    )(factors, returned)


def solution(mesh):
    placed = (
        P(("dp", "expert"), None),
        P(("dp", "expert"), None),
        P(("dp", "expert"), None),
        P("expert", "dp", None),
        P("expert", "dp", None),
        P("expert", None, "dp"),
    )
    return jax.shard_map(
        per_device, mesh=mesh, in_specs=placed, out_specs=P(("dp", "expert"), None), check_vma=False
    )
```

```python
import jax
import jax.numpy as jnp
from jax import lax
from jax.experimental import pallas as pl
from jax.experimental.pallas import tpu as pltpu
from jax.sharding import PartitionSpec as P

F32 = jnp.float32
BF16 = jnp.bfloat16


def dot(a, b, dims=((1,), (0,))):
    return lax.dot_general(a, b, (dims, ((), ())), preferred_element_type=F32)


def dispatch_kernel(routes, gates, tokens, outgoing, factors, *, capacity):
    slots = outgoing.shape[0]
    count = tokens.shape[0]
    top = routes.shape[0]
    slot = lax.broadcasted_iota(jnp.int32, (slots, count), 0)
    owner = slot // capacity
    place = (slot - owner * capacity).astype(F32)
    member = jnp.zeros((slots, count), F32)
    weight = jnp.zeros((slots, count), F32)
    for k in range(top):
        named = routes[k : k + 1, :] == owner
        member = jnp.where(named, 1.0, member)
        weight = jnp.where(named, gates[k : k + 1, :], weight)
    earlier = lax.broadcasted_iota(jnp.int32, (count, count), 0) < lax.broadcasted_iota(
        jnp.int32, (count, count), 1
    )
    rank = dot(member.astype(BF16), jnp.where(earlier, 1.0, 0.0).astype(BF16))
    chosen = jnp.where(rank == place, member, 0.0)
    outgoing[...] = dot(chosen.astype(BF16), tokens[...]).astype(BF16)
    weight = jnp.transpose(chosen * weight)
    rounded = weight.astype(BF16)
    factors[:count, :] = rounded
    factors[count:, :] = (weight - rounded.astype(F32)).astype(BF16)


def expert_kernel(side, x, weights, produced, gate, up, down, hidden, out, sems, *, wide, shard):
    members = weights.shape[0]
    inner = weights.shape[3]
    features = produced.shape[1]
    mine = side[0]
    sem = [0]

    def begin(source, target):
        copy = pltpu.make_async_copy(source, target, sems.at[sem[0]])
        sem[0] += 1
        copy.start()
        return copy

    def fetch(p, target, first, size):
        return [
            begin(
                weights.at[:, s, p * shard : (p + 1) * shard, first : first + size],
                target.at[
                    pl.ds((mine if s == 0 else 1 - mine) * members, members), :, first : first + size
                ],
            )
            for s in range(2)
        ]

    blocks = []
    for first in range(0, inner, wide):
        blocks.append(fetch(0, gate, first, wide) + fetch(1, up, first, wide))
    last = fetch(2, down, 0, inner)
    for n, first in enumerate(range(0, inner, wide)):
        columns = slice(first, first + wide)
        for copy in blocks[n]:
            copy.wait()
        gated = dot(x[...], gate[:, :, columns].reshape(2 * members * shard, wide))
        upward = dot(x[...], up[:, :, columns].reshape(2 * members * shard, wide))
        hidden[:, columns] = (gated / (1.0 + jnp.exp(-gated)) * upward).astype(BF16)
    for copy in last:
        copy.wait()
    step = wide // shard
    leaving = []
    for m in range(features // wide):
        columns = slice(m * wide, (m + 1) * wide)
        part = down[m * step : (m + 1) * step].reshape(wide, inner)
        out[:, columns] = dot(hidden[...], part, ((1,), (1,))).astype(BF16)
        leaving.append(begin(out.at[:, columns], produced.at[:, columns]))
    for copy in leaving:
        copy.wait()


def combine_kernel(factors, returned, mixture):
    count = mixture.shape[0]
    sums = dot(factors[...], returned[...])
    mixture[...] = (sums[:count] + sums[count:]).astype(BF16)


def per_device(tokens, routes, gate_values, gate_weight, up_weight, down_weight):
    groups = lax.axis_size("expert")
    shards = lax.axis_size("dp")
    count, features = tokens.shape
    top = routes.shape[1]
    capacity = 2 * count * top // groups
    slots = groups * capacity
    _, shard, inner = gate_weight.shape
    half = shards // 2
    joined = jnp.concatenate([gate_weight[0], up_weight[0], down_weight[0].T], axis=0)
    swap = [(d, (d + half) % shards) for d in range(shards)]
    other = lax.ppermute(joined, "dp", swap)
    outgoing, factors = pl.pallas_call(
        lambda *refs: dispatch_kernel(*refs, capacity=capacity),
        out_shape=(
            jax.ShapeDtypeStruct((slots, features), BF16),
            jax.ShapeDtypeStruct((2 * count, slots), BF16),
        ),
        name="dispatch",
    )(routes.T, gate_values.T, tokens)
    other, outgoing = lax.optimization_barrier((other, outgoing))
    sides = [list(range(half)), list(range(half, shards))]
    both = jnp.stack([joined, other])
    weights = lax.all_gather(both, "dp", axis=0, axis_index_groups=sides)
    side = (lax.axis_index("dp") // half).astype(jnp.int32).reshape(1)

    circles = [
        [
            ((b if e < groups // 2 else 1 - b) * half + i) * groups + e
            for e in range(groups)
        ]
        for b in range(2)
        for i in range(half)
    ]

    def exchange(rows):
        blocks = rows.reshape(groups, capacity, features)
        moved = lax.all_to_all(
            blocks,
            ("dp", "expert"),
            split_axis=0,
            concat_axis=0,
            tiled=True,
            axis_index_groups=circles,
        )
        return pltpu.with_memory_space_constraint(moved.reshape(slots, features), pltpu.VMEM)

    arrived = exchange(outgoing)
    wide = 256
    anywhere = pl.BlockSpec(memory_space=pl.ANY)
    near = pl.BlockSpec(memory_space=pltpu.VMEM)
    blocks = inner // wide
    anywhere = pl.BlockSpec(memory_space=pl.ANY)
    near = pl.BlockSpec(memory_space=pltpu.VMEM)
    blocks = inner // wide
    produced = pl.pallas_call(
        lambda *refs: expert_kernel(*refs, wide=wide, shard=shard),
        out_shape=jax.ShapeDtypeStruct((slots, features), BF16),
        in_specs=[pl.BlockSpec(memory_space=pltpu.SMEM), near, anywhere],
        out_specs=anywhere,
        scratch_shapes=[
            pltpu.VMEM((shards, shard, inner), BF16),
            pltpu.VMEM((shards, shard, inner), BF16),
            pltpu.VMEM((shards, shard, inner), BF16),
            pltpu.VMEM((slots, inner), BF16),
            pltpu.VMEM((slots, features), BF16),
            pltpu.SemaphoreType.DMA((4 * blocks + 2 + features // wide,)),
        ],
        name="expert",
    )(side, arrived, weights)
    returned = exchange(produced)
    return pl.pallas_call(
        combine_kernel,
        out_shape=jax.ShapeDtypeStruct((count, features), BF16),
        name="combine",
    )(pltpu.with_memory_space_constraint(factors, pltpu.VMEM), returned)


def solution(mesh):
    placed = (
        P(("dp", "expert"), None),
        P(("dp", "expert"), None),
        P(("dp", "expert"), None),
        P("expert", "dp", None),
        P("expert", "dp", None),
        P("expert", None, "dp"),
    )
    return jax.shard_map(
        per_device, mesh=mesh, in_specs=placed, out_specs=P(("dp", "expert"), None), check_vma=False
    )
```
